512 devices in a mesh: seq: 16 (over y, core), doc: 32 (over z, x).
Axes of the slice: x: 4, y: 8, z: 8, core: 2. Of those that a mesh axis runs over, the one named last changes fastest.
Arguments:
- queries: bfloat16 [262144, 512], P(('doc', 'seq')), parts along dimension 0, may hold values from -64 to 64
- keys: bfloat16 [262144, 512], P(('doc', 'seq')), parts along dimension 0, may hold values from -6 to 6
- values: bfloat16 [262144, 512], P(('doc', 'seq')), parts along dimension 0, may hold values from -6 to 6
- rates: float32 [262144], P(('doc', 'seq')), parts along dimension 0, may hold values from 0.1 to 1
- lengths: int32 [128], P('doc'), parts along dimension 0, may hold values from 1 to 4096, 8192 in all
- norm_gain: float32 [16384], P('doc'), parts along dimension 0, may hold values from 0.5 to 1.5
- w_gate: bfloat16 [16384, 512], P('doc'), parts along dimension 0, may hold values from -0.25 to 0.25
- w_up: bfloat16 [16384, 512], P('doc'), parts along dimension 0, may hold values from -0.25 to 0.25
- w_down: bfloat16 [16384, 512], P('doc'), parts along dimension 0, may hold values from -0.25 to 0.25
- mom_gate: float32 [16384, 512], P('doc', 'seq'), parts along dimension 0, may hold values from -3 to 3
- mom_up: float32 [16384, 512], P('doc', 'seq'), parts along dimension 0, may hold values from -3 to 3
- mom_down: float32 [16384, 512], P('doc', 'seq'), parts along dimension 0, may hold values from -3 to 3
Outputs:
- mixed: bfloat16 [262144, 512], P(('doc', 'seq')), parts along dimension 0
- new_mom_gate: float32 [16384, 512], P('doc', 'seq'), parts along dimension 0
- new_mom_up: float32 [16384, 512], P('doc', 'seq'), parts along dimension 0
- new_mom_down: float32 [16384, 512], P('doc', 'seq'), parts along dimension 0
The draws below stay inside these ranges and needn't reach their ends.
There are 32 independent parts, one for each index of `doc`. The reference program is written for one: setup_inputs(seed, part) draws one part's arguments, and reference() takes and returns one part's arrays. A program takes and returns all parts, laid end to end along the dimension named above; each array names one. Nothing has to cross between parts.
All inputs are finite; a program needn't handle non-finite values.
Results may differ from the reference program's by a relative error of at most 0.019.
Values may be sent and summed in bfloat16 or wider, within the bound.
No kernel may reach another device: no remote copies, remote signals or barrier semaphores. Data moves between devices by JAX's collectives and lax.ppermute only.
A program may use at most 64 MiB of HBM per device.

```python
import math
import jax
import jax.numpy as jnp
import numpy as np
from jax import lax

DH = 512
FH = 512
WIN = 1024
NDOCS = 4
TOK_DEV = 512
TOKENS = 8192
MOSTDOC = 4096
N_SEQ = 16


def common_keys(key):
    base = jnp.clip(jax.random.normal(jax.random.fold_in(key, 11), (TOKENS, DH), jnp.float32), -4.5, 4.5)
    return base


def draw_keys(key, part):
    return common_keys(key).astype(jnp.bfloat16)


def draw_queries(key, part):
    drawn = jnp.clip(jax.random.normal(jax.random.fold_in(key, 13), (TOKENS, DH), jnp.float32), -4.5, 4.5)
    return drawn.astype(jnp.bfloat16)


def levels(own_key, extent, shards, low, largest):
    def one(dim, blocks):
        draws = jax.random.uniform(jax.random.fold_in(jax.random.fold_in(own_key, 6), dim), (blocks,), jnp.float32, low / len(shards), largest / len(shards))
        return jnp.repeat(jnp.exp(draws), extent[dim] // blocks).reshape((-1,) + (1,) * (len(extent) - dim - 1))

    factor_of = one(*shards[0])
    for cut in shards[1:]:
        factor_of = factor_of * one(*cut)
    return factor_of


def profile(number_of, total, bound, lean):
    weights = [(1 << 20) // math.isqrt(grade ** lean) + 1 for grade in range(2, number_of + 1)]
    spare, holding = total - bound - (number_of - 1), [1] * (number_of - 1)
    while spare > 0:
        movable = [i for i in range(number_of - 1) if holding[i] < bound]
        mass, remaining = sum([weights[i] for i in movable]), spare
        for i in movable:
            more = min(bound - holding[i], max(1, remaining * weights[i] // mass), spare)
            holding[i] = holding[i] + more
            spare = spare - more
    return np.array([bound] + holding)


def ragged_sizes(key, amount, total, reach, skew):
    if amount == 2:
        one = jax.random.randint(key, (), max(1, total - reach), min(reach, total - 1) + 1)
        return jnp.stack([one, total - one])
    tallies = jnp.asarray(profile(amount, total, reach, skew), jnp.int32)
    couples = (amount - 1) // 2
    source_of, taker = tallies[1:1 + 2 * couples:2], tallies[2:2 + 2 * couples:2]
    room = jnp.minimum(source_of - 1, reach - taker)
    passed = jax.random.randint(jax.random.fold_in(key, 1), (couples,), 0, 1 << 20) % (room + 1)
    tallies = tallies.at[1:1 + 2 * couples:2].set(source_of - passed).at[2:2 + 2 * couples:2].set(taker + passed)
    return tallies[jax.random.permutation(jax.random.fold_in(key, 2), amount)]


def scatter_about(own_key, dims, deviation, reach, shards=(), kind=jnp.bfloat16):
    drawn = jax.random.normal(own_key, dims, jnp.float32) * deviation
    if len(shards) > 0:
        drawn = levels(own_key, dims, shards, -0.22, 0.18) * drawn
    return jnp.clip(drawn, min=-reach, max=reach).astype(kind)


def setup_inputs(seed: int = 0, part: int = 0) -> dict:
    key_list = jax.random.split(jax.random.key(seed), 13)
    part_keys = jax.random.split(jax.random.fold_in(key_list[12], part), 13)
    return {
        "queries": draw_queries(jax.random.fold_in(jax.random.fold_in(key_list[12], part), 71), part),
        "keys": draw_keys(jax.random.fold_in(jax.random.fold_in(key_list[12], part), 71), part),
        "values": scatter_about(part_keys[2], (TOKENS, DH), 1.0, 6.0, ((0, 16),)),
        "rates": jnp.clip(jnp.exp(math.log(1.0) - 2.3025851 * jax.random.uniform(part_keys[3], (TOKENS,), jnp.float32) ** levels(part_keys[3], (TOKENS,), ((0, 16),), -0.2, 0.2)), 0.1, 1.0),
        "lengths": ragged_sizes(part_keys[4], NDOCS, TOKENS, MOSTDOC, 2).astype(jnp.int32),
        "norm_gain": jnp.clip(1.0 + 0.1 * jax.random.normal(part_keys[5], (DH,), jnp.float32), 0.5, 1.5),
        "w_gate": scatter_about(part_keys[6], (DH, FH), DH ** -0.5, 0.25),
        "w_up": scatter_about(part_keys[7], (DH, FH), DH ** -0.5, 0.25),
        "w_down": scatter_about(part_keys[8], (FH, DH), FH ** -0.5, 0.25),
        "mom_gate": scatter_about(part_keys[9], (DH, FH), 0.2, 3.0, ((1, 16),), jnp.float32),
        "mom_up": scatter_about(part_keys[10], (DH, FH), 0.2, 3.0, ((1, 16),), jnp.float32),
        "mom_down": scatter_about(part_keys[11], (FH, DH), 0.2, 3.0, ((1, 16),), jnp.float32),
    }


momentum_decay = 0.9
step_size = 0.5

def doc_ids(positions, ends):
    return lax.optimization_barrier(jnp.sum((positions[:, None] >= ends[None, :]).astype(jnp.int32), axis=1))

def window_attention(qblk, kblk, vblk, qpos, kpos, ends):
    scores = jnp.dot(qblk, kblk.T, preferred_element_type=jnp.float32) * qblk.shape[1] ** (-0.5)
    same = doc_ids(qpos, ends)[:, None] == doc_ids(kpos, ends)[None, :]
    delta = qpos[:, None] - kpos[None, :]
    live = same & (delta >= 0) & (delta < WIN) & (kpos[None, :] >= 0)
    scores = jnp.where(live, scores, jnp.float32(-1e+30))
    top = lax.optimization_barrier(jnp.max(scores, axis=1, keepdims=True))
    weights = jnp.where(live, jnp.exp(scores - top), jnp.float32(0.0))
    total = lax.optimization_barrier(jnp.sum(weights, axis=1, keepdims=True))
    probs = (weights / total).astype(jnp.bfloat16)
    return jnp.dot(probs, vblk, preferred_element_type=jnp.float32)

def silu_parts(gate):
    sig = jax.nn.sigmoid(gate)
    return (gate * sig, sig * (1.0 + gate * (1.0 - sig)))

def step_weight(weight, moment):
    normed = moment * lax.rsqrt(lax.optimization_barrier(jnp.sum(moment * moment, axis=0, keepdims=True)) + 1e-06)
    return (weight.astype(jnp.float32) - step_size * normed).astype(jnp.bfloat16)

def rounded_sum(left, right):
    width_left = left.shape[1]
    width_right = right.shape[1]
    left_blocks = left.reshape(N_SEQ, TOK_DEV, width_left)
    right_blocks = right.reshape(N_SEQ, TOK_DEV, width_right)

    def partial_term(pair):
        term = jnp.dot(pair[0].T, pair[1], preferred_element_type=jnp.float32).astype(jnp.bfloat16)
        term = lax.optimization_barrier(term)
        return term.astype(jnp.float32)
    terms = lax.map(partial_term, (left_blocks, right_blocks))
    return lax.optimization_barrier(jnp.sum(terms, axis=0))

def reference(queries, keys, values, rates, lengths, norm_gain, w_gate, w_up, w_down, mom_gate, mom_up, mom_down):
    tokens, width = queries.shape
    ends = jnp.cumsum(lengths).astype(jnp.int32)
    block = min(512, tokens)
    padk = jnp.concatenate([jnp.zeros((WIN, width), keys.dtype), keys], 0)
    padv = jnp.concatenate([jnp.zeros((WIN, width), values.dtype), values], 0)

    def attend(number):
        start = (number * block).astype(jnp.int32)
        qblk = lax.dynamic_slice_in_dim(queries, start, block, 0)
        kblk = lax.dynamic_slice_in_dim(padk, start, block + WIN, 0)
        vblk = lax.dynamic_slice_in_dim(padv, start, block + WIN, 0)
        qpos = start + jnp.arange(block, dtype=jnp.int32)
        kpos = start - WIN + jnp.arange(block + WIN, dtype=jnp.int32)
        return window_attention(qblk, kblk, vblk, qpos, kpos, ends)
    attn = lax.map(attend, jnp.arange(tokens // block, dtype=jnp.int32)).reshape(tokens, width)
    gate = jnp.dot(keys, w_gate, preferred_element_type=jnp.float32)
    upper = jnp.dot(keys, w_up, preferred_element_type=jnp.float32)
    act, slope = silu_parts(gate)
    hidden = (act * upper).astype(jnp.bfloat16)
    err = (-(rates[:, None] * values.astype(jnp.float32))).astype(jnp.bfloat16)
    back = jnp.dot(err, w_down.T, preferred_element_type=jnp.float32)
    d_up = (back * act).astype(jnp.bfloat16)
    d_gate = (back * upper * slope).astype(jnp.bfloat16)
    scale = float(tokens) ** (-0.5)
    g_gate = rounded_sum(keys, d_gate) * scale
    g_up = rounded_sum(keys, d_up) * scale
    g_down = rounded_sum(hidden, err) * scale
    new_mom_gate = momentum_decay * mom_gate + g_gate
    new_mom_up = momentum_decay * mom_up + g_up
    new_mom_down = momentum_decay * mom_down + g_down
    gate_new = step_weight(w_gate, new_mom_gate)
    up_new = step_weight(w_up, new_mom_up)
    down_new = step_weight(w_down, new_mom_down)
    qa = jnp.dot(queries, gate_new, preferred_element_type=jnp.float32)
    qb = jnp.dot(queries, up_new, preferred_element_type=jnp.float32)
    qh = (jax.nn.silu(qa) * qb).astype(jnp.bfloat16)
    fast = jnp.dot(qh, down_new, preferred_element_type=jnp.float32)
    normed = fast * lax.rsqrt(lax.optimization_barrier(jnp.mean(fast * fast, axis=1, keepdims=True)) + 1e-06) * norm_gain
    mixed = (attn + normed).astype(jnp.bfloat16)
    return (mixed, new_mom_gate, new_mom_up, new_mom_down)
```

```python
import jax
import jax.numpy as jnp
from jax import lax
from jax.sharding import PartitionSpec as P

WIN = 1024


momentum_decay = 0.9
step_size = 0.5


def shifted(block, axis, distance):
    devices = range(lax.axis_size(axis))
    route = [(i - distance, i) for i in devices if i - distance in devices]
    return lax.ppermute(block, axis, route)


def doc_ids(positions, ends):
    return jnp.sum((positions[:, None] >= ends[None, :]).astype(jnp.int32), axis=1)


def window_attention(qblk, kblk, vblk, qpos, kpos, ends):
    scores = jnp.dot(qblk, kblk.T, preferred_element_type=jnp.float32) * qblk.shape[1] ** (-0.5)
    same = doc_ids(qpos, ends)[:, None] == doc_ids(kpos, ends)[None, :]
    delta = qpos[:, None] - kpos[None, :]
    live = same & (delta >= 0) & (delta < WIN) & (kpos[None, :] >= 0)
    scores = jnp.where(live, scores, jnp.float32(-1e30))
    top = jnp.max(scores, axis=1, keepdims=True)
    weights = jnp.where(live, jnp.exp(scores - top), jnp.float32(0.0))
    total = jnp.sum(weights, axis=1, keepdims=True)
    probs = (weights / total).astype(jnp.bfloat16)
    return jnp.dot(probs, vblk, preferred_element_type=jnp.float32)


def silu_parts(gate):
    sig = jax.nn.sigmoid(gate)
    return (gate * sig, sig * (1.0 + gate * (1.0 - sig)))


PARTNER = [(i, i ^ 1) for i in range(16)]
SAME_CORE = [[c + 2 * k for k in range(8)] for c in range(2)]


def local(
    queries,
    keys,
    values,
    rates,
    lengths,
    norm_gain,
    w_gate,
    w_up,
    w_down,
    mom_gate,
    mom_up,
    mom_down,
):
    tok, width = queries.shape
    index = lax.axis_index("seq")
    ends = jnp.cumsum(lengths)
    reach = (WIN + tok - 1) // tok
    paired = jnp.stack((keys, values))
    earlier = [shifted(paired, "seq", hops) for hops in range(reach, 0, -1)]
    buffer = jnp.concatenate(earlier + [paired], axis=1)
    halo_len = reach * tok
    first = index * tok
    begin = halo_len - WIN
    qpos = first + 0 + jnp.arange(tok, dtype=jnp.int32)
    kpos = first + 0 - WIN + jnp.arange(tok + WIN, dtype=jnp.int32)
    pieces = window_attention(
        queries,
        buffer[0, begin : begin + tok + WIN],
        buffer[1, begin : begin + tok + WIN],
        qpos,
        kpos,
        ends,
    )
    gate = jnp.dot(keys, w_gate, preferred_element_type=jnp.float32)
    upper = jnp.dot(keys, w_up, preferred_element_type=jnp.float32)
    act, slope = silu_parts(gate)
    hidden = (act * upper).astype(jnp.bfloat16)
    err = (-(rates[:, None] * values.astype(jnp.float32))).astype(jnp.bfloat16)
    back = jnp.dot(err, w_down.T, preferred_element_type=jnp.float32)
    d_up = (back * act).astype(jnp.bfloat16)
    d_gate = (back * upper * slope).astype(jnp.bfloat16)
    parts = [
        lax.dot_general(x, y, (((0,), (0,)), ((), ())), preferred_element_type=jnp.float32)
        .astype(jnp.bfloat16)
        .reshape(8, 2, 32, width)
        for x, y in ((d_gate, keys), (d_up, keys), (err, hidden))
    ]
    parts = jnp.concatenate(parts, axis=2)
    core = index % 2
    mine = lax.dynamic_index_in_dim(parts, core, 1, keepdims=False)
    other = lax.dynamic_index_in_dim(parts, 1 - core, 1, keepdims=False)
    got = lax.ppermute(other, "seq", PARTNER)
    both = (mine.astype(jnp.float32) + got.astype(jnp.float32)).astype(jnp.bfloat16)
    came = lax.all_to_all(both, "seq", 0, 0, axis_index_groups=SAME_CORE)
    total = jnp.sum(came.astype(jnp.float32), axis=0)
    scale = float(tok * lax.axis_size("seq")) ** (-0.5)
    cols = mom_gate.shape[1]
    moms = jnp.concatenate((mom_gate.T, mom_up.T, mom_down.T), axis=0)
    weights = jnp.concatenate(
        [lax.dynamic_slice_in_dim(w, index * cols, cols, 1).T for w in (w_gate, w_up, w_down)], axis=0
    )
    new_moms = momentum_decay * moms + total * scale
    new_mom_gate, new_mom_up, new_mom_down = [
        new_moms[k * cols : (k + 1) * cols].T for k in range(3)
    ]
    normed = new_moms * lax.rsqrt(jnp.sum(new_moms * new_moms, axis=1, keepdims=True) + 1e-06)
    shard = (weights.astype(jnp.float32) - step_size * normed).astype(jnp.bfloat16)
    spread = jnp.broadcast_to(shard[None], (8,) + shard.shape)
    spread = lax.all_to_all(spread, "seq", 0, 0, axis_index_groups=SAME_CORE)
    swapped = lax.ppermute(spread, "seq", PARTNER)
    pair = jnp.stack(
        (jnp.where(core == 0, spread, swapped), jnp.where(core == 0, swapped, spread)), axis=1
    )
    gate_new, up_new, down_new = [
        pair[:, :, k * cols : (k + 1) * cols].reshape(width, width).T for k in range(3)
    ]
    qa = jnp.dot(queries, gate_new, preferred_element_type=jnp.float32)
    qb = jnp.dot(queries, up_new, preferred_element_type=jnp.float32)
    qh = (jax.nn.silu(qa) * qb).astype(jnp.bfloat16)
    fast = jnp.dot(qh, down_new, preferred_element_type=jnp.float32)
    normed = fast * lax.rsqrt(jnp.mean(fast * fast, axis=1, keepdims=True) + 1e-06) * norm_gain
    mixed = (pieces + normed).astype(jnp.bfloat16)
    return (mixed, new_mom_gate, new_mom_up, new_mom_down)


def solution(mesh):
    in_specs = (
        P(("doc", "seq"), None),
        P(("doc", "seq"), None),
        P(("doc", "seq"), None),
        P(("doc", "seq")),
        P("doc"),
        P("doc"),
        P("doc", None),
        P("doc", None),
        P("doc", None),
        P("doc", "seq"),
        P("doc", "seq"),
        P("doc", "seq"),
    )
    out_specs = (P(("doc", "seq"), None), P("doc", "seq"), P("doc", "seq"), P("doc", "seq"))
    return jax.shard_map(local, mesh=mesh, in_specs=in_specs, out_specs=out_specs, check_vma=False)
```

```python
import jax
import jax.numpy as jnp
from jax import lax
from jax.experimental import pallas as pl
from jax.experimental.pallas import tpu as pltpu
from jax.sharding import PartitionSpec as P

WIN = 1024
TOK = 512
CHIPS = 8
COLS = 32
PART = 3 * COLS

momentum_decay = 0.9
step_size = 0.5

PARTNER = [(i, i ^ 1) for i in range(2 * CHIPS)]
NEXT_CHIP = [(i, i + 2) for i in range(2 * CHIPS - 2)]
SAME_CORE = [[c + 2 * k for k in range(CHIPS)] for c in range(2)]

f32 = jnp.float32
bf16 = jnp.bfloat16


def contract(x, y, dims):
    return lax.dot_general(x, y, ((dims[:1], dims[1:]), ((), ())), preferred_element_type=f32)


def grads_kernel(core, keys, values, rates, w_gate, w_up, w_down, mine, other):
    k = keys[...]
    per_token = jnp.broadcast_to(rates[...], (128, TOK)).T
    err = jnp.concatenate(
        [-(per_token * values[:, i : i + 128].astype(f32)) for i in range(0, TOK, 128)], axis=1
    ).astype(bf16)
    gate = contract(k, w_gate[...], (1, 0))
    upper = contract(k, w_up[...], (1, 0))
    back = contract(err, w_down[...], (1, 1))
    sig = jax.nn.sigmoid(gate)
    act = gate * sig
    slope = sig * (1.0 + gate * (1.0 - sig))
    hidden = (act * upper).astype(bf16)
    d_up = (back * act).astype(bf16)
    d_gate = (back * upper * slope).astype(bf16)
    for n, (x, y) in enumerate(((d_gate, k), (d_up, k), (err, hidden))):
        part = contract(x, y, (0, 0)).astype(bf16)
        rows = slice(n * COLS, (n + 1) * COLS)
        halves = [
            [part[(2 * d + c) * COLS : (2 * d + c + 1) * COLS] for d in range(CHIPS)] for c in range(2)
        ]
        for c in range(2):

            @pl.when(core[0] == c)
            def _():
                for d in range(CHIPS):
                    mine[d, rows] = halves[c][d]
                    other[d, rows] = halves[1 - c][d]


BLOCK = 256


def attention_kernel(first, lengths, q, k2, v2, k1, v1, k0, v0, out):
    for b in range(TOK // BLOCK):
        qb = q[b * BLOCK : (b + 1) * BLOCK]
        qpos = first[0] + b * BLOCK + lax.broadcasted_iota(jnp.int32, (BLOCK, 1), 0)
        low = jnp.maximum(qpos - (WIN - 1), 0)
        end = 0
        for n in range(4):
            end = end + lengths[n]
            low = jnp.where(qpos >= end, jnp.maximum(low, end), low)
        pieces = []
        for hop, kref, vref in ((2, k2, v2), (1, k1, v1), (0, k0, v0)):
            lo = max(0, b * BLOCK - WIN + hop * TOK)
            hi = min(TOK, (b + 1) * BLOCK + hop * TOK)
            s = contract(qb, kref[lo:hi], (1, 1)) * (TOK ** (-0.5))
            kpos = first[0] - hop * TOK + lo + lax.broadcasted_iota(jnp.int32, (1, hi - lo), 1)
            s = jnp.where((kpos >= low) & (kpos <= qpos), s, -1e30)
            pieces.append((s, vref[lo:hi]))
        top = pieces[0][0].max(axis=1, keepdims=True)
        for s, _ in pieces[1:]:
            top = jnp.maximum(top, s.max(axis=1, keepdims=True))
        total = 0.0
        acc = 0.0
        for s, v in pieces:
            w = jnp.exp(s - top)
            total = total + w.sum(axis=1, keepdims=True)
            acc = acc + contract(w.astype(bf16), v, (1, 0))
        out[b * BLOCK : (b + 1) * BLOCK] = acc / total


def fast_kernel(core, q, same, swap, attn, gain, out, gate_t, up_t, down_t):
    for side, src in ((core[0], same), (1 - core[0], swap)):
        for d in range(CHIPS):
            at = pl.ds(pl.multiple_of((2 * d + side) * COLS, COLS), COLS)
            for n, dst in enumerate((gate_t, up_t, down_t)):
                dst[at, :] = src[d, n * COLS : (n + 1) * COLS]
    x = q[...]
    qa = contract(x, gate_t[...], (1, 1))
    qb = contract(x, up_t[...], (1, 1))
    qh = (qa * jax.nn.sigmoid(qa) * qb).astype(bf16)
    fast = contract(qh, down_t[...], (1, 1))
    scale = lax.rsqrt(jnp.mean(fast * fast, axis=1, keepdims=True) + 1e-06)
    out[...] = (attn[...] + fast * scale * gain[...]).astype(bf16)


def near_core(x):
    return pltpu.with_memory_space_constraint(x, pltpu.VMEM)


PARAMS = pltpu.CompilerParams(vmem_limit_bytes=24 * 2**20)
SMEM = pl.BlockSpec(memory_space=pltpu.SMEM)
VMEM = pl.BlockSpec(memory_space=pltpu.VMEM)


def local(
    queries,
    keys,
    values,
    rates,
    lengths,
    norm_gain,
    w_gate,
    w_up,
    w_down,
    mom_gate,
    mom_up,
    mom_down,
):
    index = lax.axis_index("seq")
    core = index % 2
    cores = jnp.reshape(core, (1,))
    k2 = lax.ppermute(keys, "seq", NEXT_CHIP)
    v2 = lax.ppermute(values, "seq", NEXT_CHIP)
    piece = jax.ShapeDtypeStruct((CHIPS, PART, TOK), bf16)
    mine, other = pl.pallas_call(
        grads_kernel,
        out_shape=(pltpu.VMEM(piece.shape, bf16),) * 2,
        in_specs=[SMEM] + [VMEM] * 6,
        out_specs=(VMEM, VMEM),
        compiler_params=PARAMS,
    )(cores, keys, values, rates.reshape(1, TOK), w_gate, w_up, w_down)
    got = lax.ppermute(other, "seq", PARTNER)
    both = (mine.astype(f32) + got.astype(f32)).astype(bf16)
    came = lax.all_to_all(both, "seq", 0, 0, axis_index_groups=SAME_CORE)
    near_k = lax.ppermute(jnp.where(core == 0, keys, k2), "seq", PARTNER)
    near_v = lax.ppermute(jnp.where(core == 0, values, v2), "seq", PARTNER)
    attn = pl.pallas_call(
        attention_kernel,
        out_shape=pltpu.VMEM((TOK, TOK), f32),
        in_specs=[SMEM, SMEM] + [VMEM] * 7,
        out_specs=VMEM,
        compiler_params=PARAMS,
    )(
        jnp.reshape(index * TOK, (1,)),
        lengths,
        near_core(queries),
        near_core(k2),
        near_core(v2),
        near_core(near_k),
        near_core(near_v),
        near_core(keys),
        near_core(values),
    )
    scale = float(TOK * lax.axis_size("seq")) ** (-0.5)
    total = jnp.sum(came.astype(f32), axis=0)
    moms = jnp.concatenate((mom_gate.T, mom_up.T, mom_down.T), axis=0)
    weights = jnp.concatenate(
        [lax.dynamic_slice_in_dim(w, index * COLS, COLS, 1).T for w in (w_gate, w_up, w_down)],
        axis=0,
    )
    new_moms = momentum_decay * moms + total * scale
    normed = new_moms * lax.rsqrt(jnp.sum(new_moms * new_moms, axis=1, keepdims=True) + 1e-06)
    shard = (weights.astype(f32) - step_size * normed).astype(bf16)
    spread = jnp.broadcast_to(shard[None], (CHIPS,) + shard.shape)
    same = lax.all_to_all(spread, "seq", 0, 0, axis_index_groups=SAME_CORE)
    swap = lax.ppermute(same, "seq", PARTNER)
    mixed = pl.pallas_call(
        fast_kernel,
        out_shape=jax.ShapeDtypeStruct((TOK, TOK), bf16),
        in_specs=[SMEM] + [VMEM] * 5,
        out_specs=VMEM,
        compiler_params=PARAMS,
        scratch_shapes=[pltpu.VMEM((TOK, TOK), bf16)] * 3,
    )(
        cores,
        near_core(queries),
        near_core(same),
        near_core(swap),
        near_core(attn),
        norm_gain.reshape(1, TOK),
    )
    outs = [new_moms[k * COLS : (k + 1) * COLS].T for k in range(3)]
    return (mixed, *outs)


def solution(mesh):
    in_specs = (
        P(("doc", "seq"), None),
        P(("doc", "seq"), None),
        P(("doc", "seq"), None),
        P(("doc", "seq")),
        P("doc"),
        P("doc"),
        P("doc", None),
        P("doc", None),
        P("doc", None),
        P("doc", "seq"),
        P("doc", "seq"),
        P("doc", "seq"),
    )
    out_specs = (P(("doc", "seq"), None), P("doc", "seq"), P("doc", "seq"), P("doc", "seq"))
    return jax.shard_map(local, mesh=mesh, in_specs=in_specs, out_specs=out_specs, check_vma=False)
```

```python
import jax
import jax.numpy as jnp
from jax import lax
from jax.experimental import pallas as pl
from jax.experimental.pallas import tpu as pltpu
from jax.sharding import PartitionSpec as P

WIN = 1024
TOK = 512
CHIPS = 8
COLS = 32
PART = 3 * COLS
GRAD_SCALE = float(2 * CHIPS * TOK) ** (-0.5)

momentum_decay = 0.9
step_size = 0.5

PARTNER = [(i, i ^ 1) for i in range(2 * CHIPS)]
NEXT_CHIP = [(i, i + 2) for i in range(2 * CHIPS - 2)]
SAME_CORE = [[c + 2 * k for k in range(CHIPS)] for c in range(2)]

f32 = jnp.float32
bf16 = jnp.bfloat16


def contract(x, y, dims):
    return lax.dot_general(x, y, ((dims[:1], dims[1:]), ((), ())), preferred_element_type=f32)


def grads_kernel(core, keys, values, rates, w_gate, w_up, w_down, mine, other, *refs):
    bufs, sems = refs[:5], refs[5]
    copies = [
        pltpu.make_async_copy(src, dst, sems.at[n])
        for n, (src, dst) in enumerate(zip((keys, w_gate, values, w_up, w_down), bufs))
    ]
    for copy in copies:
        copy.start()
    k_buf, gate_buf, v_buf, up_buf, down_buf = bufs
    per_token = jnp.broadcast_to(rates[...], (128, TOK)).T
    copies[0].wait()
    copies[1].wait()
    k = k_buf[...]
    gate = contract(k, gate_buf[...], (1, 0))
    copies[2].wait()
    err = jnp.concatenate(
        [-(per_token * v_buf[:, i : i + 128].astype(f32)) for i in range(0, TOK, 128)], axis=1
    ).astype(bf16)
    copies[3].wait()
    upper = contract(k, up_buf[...], (1, 0))
    copies[4].wait()
    back = contract(err, down_buf[...], (1, 1))
    sig = jax.nn.sigmoid(gate)
    act = gate * sig
    slope = sig * (1.0 + gate * (1.0 - sig))
    hidden = (act * upper).astype(bf16)
    d_up = (back * act).astype(bf16)
    d_gate = (back * upper * slope).astype(bf16)
    for n, (x, y) in enumerate(((d_gate, k), (d_up, k), (err, hidden))):
        part = contract(x, y, (0, 0)).astype(bf16)
        rows = slice(n * COLS, (n + 1) * COLS)
        halves = [
            [part[(2 * d + c) * COLS : (2 * d + c + 1) * COLS] for d in range(CHIPS)] for c in range(2)
        ]
        for c in range(2):

            @pl.when(core[0] == c)
            def _():
                for d in range(CHIPS):
                    mine[d, rows] = halves[c][d]
                    other[d, rows] = halves[1 - c][d]


def pair_kernel(mine, got, out):
    for d in range(CHIPS):
        out[d] = (mine[d].astype(f32) + got[d].astype(f32)).astype(bf16)


def update_kernel(came, *refs):
    weights, moms, news, spread = refs[0], refs[1:4], refs[4:7], refs[7]
    bufs, sems = refs[8:11], refs[11]
    copies = [pltpu.make_async_copy(moms[n], bufs[n], sems.at[n]) for n in range(3)]
    for copy in copies:
        copy.start()
    for n in range(3):
        rows = slice(n * COLS, (n + 1) * COLS)
        total = came[0, rows].astype(f32)
        for d in range(1, CHIPS):
            total = total + came[d, rows].astype(f32)
        copies[n].wait()
        new = momentum_decay * bufs[n][...] + total * GRAD_SCALE
        news[n][...] = new
        normed = new * lax.rsqrt(jnp.sum(new * new, axis=1, keepdims=True) + 1e-06)
        shard = (weights[rows].astype(f32) - step_size * normed).astype(bf16)
        for d in range(CHIPS):
            spread[d, rows] = shard


BLOCK = 256


def attention_kernel(
    first, lengths, q, k2, v2, k1, v1, k0, v0, weights, out, out_weights
):
    out_weights[...] = weights[...]
    for b in range(TOK // BLOCK):
        qb = q[b * BLOCK : (b + 1) * BLOCK]
        qpos = first[0] + b * BLOCK + lax.broadcasted_iota(jnp.int32, (BLOCK, 1), 0)
        low = jnp.maximum(qpos - (WIN - 1), 0)
        end = 0
        for n in range(4):
            end = end + lengths[n]
            low = jnp.where(qpos >= end, jnp.maximum(low, end), low)
        pieces = []
        for hop, kref, vref in ((2, k2, v2), (1, k1, v1), (0, k0, v0)):
            lo = max(0, b * BLOCK - WIN + hop * TOK)
            hi = min(TOK, (b + 1) * BLOCK + hop * TOK)
            s = contract(qb, kref[lo:hi], (1, 1)) * (TOK ** (-0.5))
            kpos = first[0] - hop * TOK + lo + lax.broadcasted_iota(jnp.int32, (1, hi - lo), 1)
            s = jnp.where((kpos >= low) & (kpos <= qpos), s, -1e30)
            pieces.append((s, vref[lo:hi]))
        top = pieces[0][0].max(axis=1, keepdims=True)
        for s, _ in pieces[1:]:
            top = jnp.maximum(top, s.max(axis=1, keepdims=True))
        total = 0.0
        acc = 0.0
        for s, v in pieces:
            w = jnp.exp(s - top)
            total = total + w.sum(axis=1, keepdims=True)
            acc = acc + contract(w.astype(bf16), v, (1, 0))
        out[b * BLOCK : (b + 1) * BLOCK] = acc / total


def fast_kernel(core, q, same, swap, attn, gain, out, gate_t, up_t, down_t):
    for side, src in ((core[0], same), (1 - core[0], swap)):
        for d in range(CHIPS):
            at = pl.ds(pl.multiple_of((2 * d + side) * COLS, COLS), COLS)
            for n, dst in enumerate((gate_t, up_t, down_t)):
                dst[at, :] = src[d, n * COLS : (n + 1) * COLS]
    x = q[...]
    qa = contract(x, gate_t[...], (1, 1))
    qb = contract(x, up_t[...], (1, 1))
    qh = (qa * jax.nn.sigmoid(qa) * qb).astype(bf16)
    fast = contract(qh, down_t[...], (1, 1))
    scale = lax.rsqrt(jnp.mean(fast * fast, axis=1, keepdims=True) + 1e-06)
    out[...] = (attn[...] + fast * scale * gain[...]).astype(bf16)


def near_core(x):
    return pltpu.with_memory_space_constraint(x, pltpu.VMEM)


def far(x):
    return pltpu.with_memory_space_constraint(x, pltpu.HBM)


PARAMS = pltpu.CompilerParams(vmem_limit_bytes=24 * 2**20)
SMEM = pl.BlockSpec(memory_space=pltpu.SMEM)
VMEM = pl.BlockSpec(memory_space=pltpu.VMEM)
HBM = pl.BlockSpec(memory_space=pltpu.HBM)


def local(
    queries,
    keys,
    values,
    rates,
    lengths,
    norm_gain,
    w_gate,
    w_up,
    w_down,
    mom_gate,
    mom_up,
    mom_down,
):
    index = lax.axis_index("seq")
    core = index % 2
    cores = jnp.reshape(core, (1,))
    k2 = lax.ppermute(keys, "seq", NEXT_CHIP)
    v2 = lax.ppermute(values, "seq", NEXT_CHIP)
    piece = jax.ShapeDtypeStruct((CHIPS, PART, TOK), bf16)
    mine, other = pl.pallas_call(
        grads_kernel,
        out_shape=(pltpu.VMEM(piece.shape, bf16),) * 2,
        in_specs=[SMEM, HBM, HBM, VMEM, HBM, HBM, HBM],
        out_specs=(VMEM, VMEM),
        scratch_shapes=[pltpu.VMEM((TOK, TOK), bf16)] * 5 + [pltpu.SemaphoreType.DMA((5,))],
        compiler_params=PARAMS,
    )(cores, far(keys), far(values), rates.reshape(1, TOK), far(w_gate), far(w_up), far(w_down))
    got = lax.ppermute(other, "seq", PARTNER)
    both = pl.pallas_call(
        pair_kernel,
        out_shape=pltpu.VMEM(piece.shape, bf16),
        in_specs=[VMEM] * 2,
        out_specs=VMEM,
        compiler_params=PARAMS,
    )(near_core(mine), near_core(got))
    came = lax.all_to_all(both, "seq", 0, 0, axis_index_groups=SAME_CORE)
    near_k = lax.ppermute(jnp.where(core == 0, keys, k2), "seq", PARTNER)
    near_v = lax.ppermute(jnp.where(core == 0, values, v2), "seq", PARTNER)
    weights = [lax.dynamic_slice_in_dim(w, index * COLS, COLS, 1) for w in (w_gate, w_up, w_down)]
    weights = jnp.concatenate(weights, axis=1).T
    attn, weights = pl.pallas_call(
        attention_kernel,
        out_shape=(
            jax.ShapeDtypeStruct((TOK, TOK), f32),
            pltpu.VMEM((PART, TOK), bf16),
        ),
        in_specs=[SMEM, SMEM] + [VMEM] * 8,
        out_specs=(VMEM,) * 2,
        compiler_params=PARAMS,
    )(
        jnp.reshape(index * TOK, (1,)),
        lengths,
        near_core(queries),
        near_core(k2),
        near_core(v2),
        near_core(near_k),
        near_core(near_v),
        near_core(keys),
        near_core(values),
        weights,
    )
    *news, spread = pl.pallas_call(
        update_kernel,
        out_shape=(jax.ShapeDtypeStruct((COLS, TOK), f32),) * 3 + (pltpu.VMEM(piece.shape, bf16),),
        in_specs=[VMEM] * 2 + [HBM] * 3,
        out_specs=(VMEM,) * 4,
        scratch_shapes=[pltpu.VMEM((COLS, TOK), f32)] * 3 + [pltpu.SemaphoreType.DMA((3,))],
        compiler_params=PARAMS,
    )(near_core(came), near_core(weights), far(mom_gate.T), far(mom_up.T), far(mom_down.T))
    same = lax.all_to_all(spread, "seq", 0, 0, axis_index_groups=SAME_CORE)
    swap = lax.ppermute(same, "seq", PARTNER)
    mixed = pl.pallas_call(
        fast_kernel,
        out_shape=jax.ShapeDtypeStruct((TOK, TOK), bf16),
        in_specs=[SMEM] + [VMEM] * 5,
        out_specs=VMEM,
        compiler_params=PARAMS,
        scratch_shapes=[pltpu.VMEM((TOK, TOK), bf16)] * 3,
    )(
        cores,
        near_core(queries),
        near_core(same),
        near_core(swap),
        near_core(attn),
        norm_gain.reshape(1, TOK),
    )
    return (mixed, *[new.T for new in news])


def solution(mesh):
    in_specs = (
        P(("doc", "seq"), None),
        P(("doc", "seq"), None),
        P(("doc", "seq"), None),
        P(("doc", "seq")),
        P("doc"),
        P("doc"),
        P("doc", None),
        P("doc", None),
        P("doc", None),
        P("doc", "seq"),
        P("doc", "seq"),
        P("doc", "seq"),
    )
    out_specs = (P(("doc", "seq"), None), P("doc", "seq"), P("doc", "seq"), P("doc", "seq"))
    return jax.shard_map(local, mesh=mesh, in_specs=in_specs, out_specs=out_specs, check_vma=False)
```

```python
import jax
import jax.numpy as jnp
from jax import lax
from jax.experimental import pallas as pl
from jax.experimental.pallas import tpu as pltpu
from jax.sharding import PartitionSpec as P

WIN = 1024
TOK = 512
CHIPS = 8
COLS = 32
PART = 3 * COLS
GRAD_SCALE = float(2 * CHIPS * TOK) ** (-0.5)

momentum_decay = 0.9
step_size = 0.5

PARTNER = [(i, i ^ 1) for i in range(2 * CHIPS)]
NEXT_CHIP = [(i, i + 2) for i in range(2 * CHIPS - 2)]
SAME_CORE = [[c + 2 * k for k in range(CHIPS)] for c in range(2)]

f32 = jnp.float32
bf16 = jnp.bfloat16


def contract(x, y, dims):
    return lax.dot_general(x, y, ((dims[:1], dims[1:]), ((), ())), preferred_element_type=f32)


def grads_kernel(core, keys, values, rates, w_gate, w_up, w_down, mine, other, *refs):
    bufs, sems = refs[:6], refs[6]
    copies = [
        pltpu.make_async_copy(src, dst, sems.at[n])
        for n, (src, dst) in enumerate(zip((keys, w_gate, rates, values, w_up, w_down), bufs))
    ]
    for copy in copies:
        copy.start()
    k_buf, gate_buf, rate_buf, v_buf, up_buf, down_buf = bufs
    copies[0].wait()
    copies[1].wait()
    k = k_buf[...]
    gate = contract(k, gate_buf[...], (1, 0))
    copies[2].wait()
    per_token = jnp.broadcast_to(rate_buf[...], (128, TOK)).T
    copies[3].wait()
    err = jnp.concatenate(
        [-(per_token * v_buf[:, i : i + 128].astype(f32)) for i in range(0, TOK, 128)], axis=1
    ).astype(bf16)
    copies[4].wait()
    upper = contract(k, up_buf[...], (1, 0))
    copies[5].wait()
    back = contract(err, down_buf[...], (1, 1))
    sig = jax.nn.sigmoid(gate)
    act = gate * sig
    slope = sig * (1.0 + gate * (1.0 - sig))
    hidden = (act * upper).astype(bf16)
    d_up = (back * act).astype(bf16)
    d_gate = (back * upper * slope).astype(bf16)
    for n, (x, y) in enumerate(((d_gate, k), (d_up, k), (err, hidden))):
        part = contract(x, y, (0, 0)).astype(bf16)
        rows = slice(n * COLS, (n + 1) * COLS)
        halves = [
            [part[(2 * d + c) * COLS : (2 * d + c + 1) * COLS] for d in range(CHIPS)] for c in range(2)
        ]
        for c in range(2):

            @pl.when(core[0] == c)
            def _():
                for d in range(CHIPS):
                    mine[d, rows] = halves[c][d]
                    other[d, rows] = halves[1 - c][d]


def pair_kernel(mine, got, out):
    for d in range(CHIPS):
        out[d] = (mine[d].astype(f32) + got[d].astype(f32)).astype(bf16)


def update_kernel(came, *refs):
    weights, moms, news, spread = refs[0], refs[1:4], refs[4:7], refs[7]
    bufs, sems = refs[8:11], refs[11]
    copies = [pltpu.make_async_copy(moms[n], bufs[n], sems.at[n]) for n in range(3)]
    for copy in copies:
        copy.start()
    for n in range(3):
        rows = slice(n * COLS, (n + 1) * COLS)
        total = came[0, rows].astype(f32)
        for d in range(1, CHIPS):
            total = total + came[d, rows].astype(f32)
        copies[n].wait()
        new = momentum_decay * bufs[n][...] + total * GRAD_SCALE
        news[n][...] = new
        normed = new * lax.rsqrt(jnp.sum(new * new, axis=1, keepdims=True) + 1e-06)
        shard = (weights[rows].astype(f32) - step_size * normed).astype(bf16)
        for d in range(CHIPS):
            spread[d, rows] = shard


BLOCK = 256


def attention_kernel(first, lengths, q, k2, v2, k1, v1, k0, v0, out):
    for b in range(TOK // BLOCK):
        qb = q[b * BLOCK : (b + 1) * BLOCK]
        qpos = first[0] + b * BLOCK + lax.broadcasted_iota(jnp.int32, (BLOCK, 1), 0)
        low = jnp.maximum(qpos - (WIN - 1), 0)
        end = 0
        for n in range(4):
            end = end + lengths[n]
            low = jnp.where(qpos >= end, jnp.maximum(low, end), low)
        pieces = []
        for hop, kref, vref in ((2, k2, v2), (1, k1, v1), (0, k0, v0)):
            lo = max(0, b * BLOCK - WIN + hop * TOK)
            hi = min(TOK, (b + 1) * BLOCK + hop * TOK)
            s = contract(qb, kref[lo:hi], (1, 1)) * (TOK ** (-0.5))
            kpos = first[0] - hop * TOK + lo + lax.broadcasted_iota(jnp.int32, (1, hi - lo), 1)
            s = jnp.where((kpos >= low) & (kpos <= qpos), s, -1e30)
            pieces.append((s, vref[lo:hi]))
        top = pieces[0][0].max(axis=1, keepdims=True)
        for s, _ in pieces[1:]:
            top = jnp.maximum(top, s.max(axis=1, keepdims=True))
        total = 0.0
        acc = 0.0
        for s, v in pieces:
            w = jnp.exp(s - top)
            total = total + w.sum(axis=1, keepdims=True)
            acc = acc + contract(w.astype(bf16), v, (1, 0))
        out[b * BLOCK : (b + 1) * BLOCK] = acc / total


def fast_kernel(core, q, same, swap, attn, gain, out, gate_t, up_t, down_t):
    for side, src in ((core[0], same), (1 - core[0], swap)):
        for d in range(CHIPS):
            at = pl.ds(pl.multiple_of((2 * d + side) * COLS, COLS), COLS)
            for n, dst in enumerate((gate_t, up_t, down_t)):
                dst[at, :] = src[d, n * COLS : (n + 1) * COLS]
    x = q[...]
    qa = contract(x, gate_t[...], (1, 1))
    qb = contract(x, up_t[...], (1, 1))
    qh = (qa * jax.nn.sigmoid(qa) * qb).astype(bf16)
    fast = contract(qh, down_t[...], (1, 1))
    scale = lax.rsqrt(jnp.mean(fast * fast, axis=1, keepdims=True) + 1e-06)
    out[...] = (attn[...] + fast * scale * gain[...]).astype(bf16)


def near_core(x):
    return pltpu.with_memory_space_constraint(x, pltpu.VMEM)


def far(x):
    return pltpu.with_memory_space_constraint(x, pltpu.HBM)


PARAMS = pltpu.CompilerParams(vmem_limit_bytes=24 * 2**20)
SMEM = pl.BlockSpec(memory_space=pltpu.SMEM)
VMEM = pl.BlockSpec(memory_space=pltpu.VMEM)
HBM = pl.BlockSpec(memory_space=pltpu.HBM)


def local(
    queries,
    keys,
    values,
    rates,
    lengths,
    norm_gain,
    w_gate,
    w_up,
    w_down,
    mom_gate,
    mom_up,
    mom_down,
):
    index = lax.axis_index("seq")
    core = index % 2
    cores = jnp.reshape(core, (1,))
    k2 = lax.ppermute(keys, "seq", NEXT_CHIP)
    v2 = lax.ppermute(values, "seq", NEXT_CHIP)
    piece = jax.ShapeDtypeStruct((CHIPS, PART, TOK), bf16)
    mine, other = pl.pallas_call(
        grads_kernel,
        out_shape=(pltpu.VMEM(piece.shape, bf16),) * 2,
        in_specs=[SMEM] + [HBM] * 6,
        out_specs=(VMEM, VMEM),
        scratch_shapes=[pltpu.VMEM((TOK, TOK), bf16)] * 2
        + [pltpu.VMEM((1, TOK), f32)]
        + [pltpu.VMEM((TOK, TOK), bf16)] * 3
        + [pltpu.SemaphoreType.DMA((6,))],
        compiler_params=PARAMS,
    )(
        cores,
        far(keys),
        far(values),
        far(rates.reshape(1, TOK)),
        far(w_gate),
        far(w_up),
        far(w_down),
    )
    got = lax.ppermute(other, "seq", PARTNER)
    both = pl.pallas_call(
        pair_kernel,
        out_shape=pltpu.VMEM(piece.shape, bf16),
        in_specs=[VMEM] * 2,
        out_specs=VMEM,
        compiler_params=PARAMS,
    )(near_core(mine), near_core(got))
    came = lax.all_to_all(both, "seq", 0, 0, axis_index_groups=SAME_CORE)
    weights = [lax.dynamic_slice_in_dim(w, index * COLS, COLS, 1) for w in (w_gate, w_up, w_down)]
    weights = jnp.concatenate(weights, axis=1).T
    *news, spread = pl.pallas_call(
        update_kernel,
        out_shape=(jax.ShapeDtypeStruct((COLS, TOK), f32),) * 3 + (pltpu.VMEM(piece.shape, bf16),),
        in_specs=[VMEM] * 2 + [HBM] * 3,
        out_specs=(VMEM,) * 4,
        scratch_shapes=[pltpu.VMEM((COLS, TOK), f32)] * 3 + [pltpu.SemaphoreType.DMA((3,))],
        compiler_params=PARAMS,
    )(near_core(came), near_core(weights), far(mom_gate.T), far(mom_up.T), far(mom_down.T))
    same = lax.all_to_all(spread, "seq", 0, 0, axis_index_groups=SAME_CORE)
    near_k = lax.ppermute(jnp.where(core == 0, keys, k2), "seq", PARTNER)
    near_v = lax.ppermute(jnp.where(core == 0, values, v2), "seq", PARTNER)
    attn = pl.pallas_call(
        attention_kernel,
        out_shape=jax.ShapeDtypeStruct((TOK, TOK), f32),
        in_specs=[SMEM, SMEM] + [VMEM] * 7,
        out_specs=VMEM,
        compiler_params=PARAMS,
    )(
        jnp.reshape(index * TOK, (1,)),
        lengths,
        near_core(queries),
        near_core(k2),
        near_core(v2),
        near_core(near_k),
        near_core(near_v),
        near_core(keys),
        near_core(values),
    )
    swap = lax.ppermute(same, "seq", PARTNER)
    mixed = pl.pallas_call(
        fast_kernel,
        out_shape=jax.ShapeDtypeStruct((TOK, TOK), bf16),
        in_specs=[SMEM] + [VMEM] * 5,
        out_specs=VMEM,
        compiler_params=PARAMS,
        scratch_shapes=[pltpu.VMEM((TOK, TOK), bf16)] * 3,
    )(
        cores,
        near_core(queries),
        near_core(same),
        near_core(swap),
        near_core(attn),
        norm_gain.reshape(1, TOK),
    )
    return (mixed, *[new.T for new in news])


def solution(mesh):
    in_specs = (
        P(("doc", "seq"), None),
        P(("doc", "seq"), None),
        P(("doc", "seq"), None),
        P(("doc", "seq")),
        P("doc"),
        P("doc"),
        P("doc", None),
        P("doc", None),
        P("doc", None),
        P("doc", "seq"),
        P("doc", "seq"),
        P("doc", "seq"),
    )
    out_specs = (P(("doc", "seq"), None), P("doc", "seq"), P("doc", "seq"), P("doc", "seq"))
    return jax.shard_map(local, mesh=mesh, in_specs=in_specs, out_specs=out_specs, check_vma=False)
```

```python
import jax
import jax.numpy as jnp
from jax import lax
from jax.experimental import pallas as pl
from jax.experimental.pallas import tpu as pltpu
from jax.sharding import PartitionSpec as P

WIN = 1024
TOK = 512
CHIPS = 8
COLS = 32
PART = 3 * COLS
GRAD_SCALE = float(2 * CHIPS * TOK) ** (-0.5)

momentum_decay = 0.9
step_size = 0.5

PARTNER = [(i, i ^ 1) for i in range(2 * CHIPS)]
NEXT_CHIP = [(i, i + 2) for i in range(2 * CHIPS - 2)]
RIGHT = [(i, (i + 2) % (2 * CHIPS)) for i in range(2 * CHIPS)]
LEFT = [(i, (i - 2) % (2 * CHIPS)) for i in range(2 * CHIPS)]
SAME_CORE = [[c + 2 * k for k in range(CHIPS)] for c in range(2)]
SAME_PARITY = [[c + 2 * (2 * k + p) for k in range(CHIPS // 2)] for p in range(2) for c in range(2)]

f32 = jnp.float32
bf16 = jnp.bfloat16


def contract(x, y, dims):
    return lax.dot_general(x, y, ((dims[:1], dims[1:]), ((), ())), preferred_element_type=f32)


def grads_kernel(core, keys, values, rates, w_gate, w_up, w_down, mine, other, *refs):
    bufs, sems = refs[:6], refs[6]
    copies = [
        pltpu.make_async_copy(src, dst, sems.at[n])
        for n, (src, dst) in enumerate(zip((keys, w_gate, rates, values, w_up, w_down), bufs))
    ]
    for copy in copies:
        copy.start()
    k_buf, gate_buf, rate_buf, v_buf, up_buf, down_buf = bufs
    copies[0].wait()
    copies[1].wait()
    k = k_buf[...]
    gate = contract(k, gate_buf[...], (1, 0))
    copies[2].wait()
    per_token = jnp.broadcast_to(rate_buf[...], (128, TOK)).T
    copies[3].wait()
    err = jnp.concatenate(
        [-(per_token * v_buf[:, i : i + 128].astype(f32)) for i in range(0, TOK, 128)], axis=1
    ).astype(bf16)
    copies[4].wait()
    upper = contract(k, up_buf[...], (1, 0))
    copies[5].wait()
    back = contract(err, down_buf[...], (1, 1))
    sig = jax.nn.sigmoid(gate)
    act = gate * sig
    slope = sig * (1.0 + gate * (1.0 - sig))
    hidden = (act * upper).astype(bf16)
    d_up = (back * act).astype(bf16)
    d_gate = (back * upper * slope).astype(bf16)
    for n, (x, y) in enumerate(((d_gate, k), (d_up, k), (err, hidden))):
        part = contract(x, y, (0, 0)).astype(bf16)
        rows = slice(n * COLS, (n + 1) * COLS)
        halves = [
            [part[(2 * d + c) * COLS : (2 * d + c + 1) * COLS] for d in range(CHIPS)] for c in range(2)
        ]
        for c in range(2):

            @pl.when(core[0] == c)
            def _():
                for d in range(CHIPS):
                    mine[d, rows] = halves[c][d]
                    other[d, rows] = halves[1 - c][d]


def pair_kernel(mine, got, out):
    for d in range(CHIPS):
        out[d] = (mine[d].astype(f32) + got[d].astype(f32)).astype(bf16)


def update_kernel(came, *refs):
    weights, moms, news, spread = refs[0], refs[1:4], refs[4:7], refs[7]
    bufs, sems = refs[8:11], refs[11]
    copies = [pltpu.make_async_copy(moms[n], bufs[n], sems.at[n]) for n in range(3)]
    for copy in copies:
        copy.start()
    for n in range(3):
        rows = slice(n * COLS, (n + 1) * COLS)
        total = came[0, rows].astype(f32)
        for d in range(1, CHIPS):
            total = total + came[d, rows].astype(f32)
        copies[n].wait()
        new = momentum_decay * bufs[n][...] + total * GRAD_SCALE
        news[n][...] = new
        normed = new * lax.rsqrt(jnp.sum(new * new, axis=1, keepdims=True) + 1e-06)
        shard = (weights[rows].astype(f32) - step_size * normed).astype(bf16)
        for d in range(CHIPS // 2):
            spread[d, rows] = shard


BLOCK = 256


def attention_kernel(first, lengths, *refs):
    out, bufs, sems = refs[7], refs[8:15], refs[15]
    copies = [pltpu.make_async_copy(refs[n], bufs[n], sems.at[n]) for n in range(7)]
    for copy in copies:
        copy.start()
    for copy in copies:
        copy.wait()
    q, k2, v2, k1, v1, k0, v0 = bufs
    for b in range(TOK // BLOCK):
        qb = q[b * BLOCK : (b + 1) * BLOCK]
        qpos = first[0] + b * BLOCK + lax.broadcasted_iota(jnp.int32, (BLOCK, 1), 0)
        low = jnp.maximum(qpos - (WIN - 1), 0)
        end = 0
        for n in range(4):
            end = end + lengths[n]
            low = jnp.where(qpos >= end, jnp.maximum(low, end), low)
        pieces = []
        for hop, kref, vref in ((2, k2, v2), (1, k1, v1), (0, k0, v0)):
            lo = max(0, b * BLOCK - WIN + hop * TOK)
            hi = min(TOK, (b + 1) * BLOCK + hop * TOK)
            s = contract(qb, kref[lo:hi], (1, 1)) * (TOK ** (-0.5))
            kpos = first[0] - hop * TOK + lo + lax.broadcasted_iota(jnp.int32, (1, hi - lo), 1)
            s = jnp.where((kpos >= low) & (kpos <= qpos), s, -1e30)
            pieces.append((s, vref[lo:hi]))
        top = pieces[0][0].max(axis=1, keepdims=True)
        for s, _ in pieces[1:]:
            top = jnp.maximum(top, s.max(axis=1, keepdims=True))
        total = 0.0
        acc = 0.0
        for s, v in pieces:
            w = jnp.exp(s - top)
            total = total + w.sum(axis=1, keepdims=True)
            acc = acc + contract(w.astype(bf16), v, (1, 0))
        out[b * BLOCK : (b + 1) * BLOCK] = acc / total


def pick_kernel(chip, same, right, left):
    at = chip[0] // 2
    for out, step in ((right, 3), (left, 1)):
        out[0] = same[at]
        out[1] = same[(at + step) % (CHIPS // 2)]


def fast_kernel(core, chip, q, same, sides, same_swap, sides_swap, attn, gain, out, *dsts):
    for side, blocks, beside in ((core[0], same, sides), (1 - core[0], same_swap, sides_swap)):
        sources = [(blocks, d, 2 * d + chip[0] % 2) for d in range(CHIPS // 2)]
        sources += [(beside, n, (chip[0] + off) % CHIPS) for n, off in enumerate((7, 5, 1, 3))]
        for src, n, owner in sources:
            at = pl.ds(pl.multiple_of((2 * owner + side) * COLS, COLS), COLS)
            for k, dst in enumerate(dsts):
                dst[at, :] = src[n, k * COLS : (k + 1) * COLS]
    gate_t, up_t, down_t = dsts
    x = q[...]
    qa = contract(x, gate_t[...], (1, 1))
    qb = contract(x, up_t[...], (1, 1))
    qh = (qa * jax.nn.sigmoid(qa) * qb).astype(bf16)
    fast = contract(qh, down_t[...], (1, 1))
    scale = lax.rsqrt(jnp.mean(fast * fast, axis=1, keepdims=True) + 1e-06)
    out[...] = (attn[...] + fast * scale * gain[...]).astype(bf16)


def near_core(x):
    return pltpu.with_memory_space_constraint(x, pltpu.VMEM)


def far(x):
    return pltpu.with_memory_space_constraint(x, pltpu.HBM)


PARAMS = pltpu.CompilerParams(vmem_limit_bytes=24 * 2**20)
SMEM = pl.BlockSpec(memory_space=pltpu.SMEM)
VMEM = pl.BlockSpec(memory_space=pltpu.VMEM)
HBM = pl.BlockSpec(memory_space=pltpu.HBM)


def local(
    queries,
    keys,
    values,
    rates,
    lengths,
    norm_gain,
    w_gate,
    w_up,
    w_down,
    mom_gate,
    mom_up,
    mom_down,
):
    index = lax.axis_index("seq")
    core = index % 2
    cores = jnp.reshape(core, (1,))
    chips = jnp.reshape(index // 2, (1,))
    k2 = lax.ppermute(keys, "seq", NEXT_CHIP)
    v2 = lax.ppermute(values, "seq", NEXT_CHIP)
    piece = jax.ShapeDtypeStruct((CHIPS, PART, TOK), bf16)
    mine, other = pl.pallas_call(
        grads_kernel,
        out_shape=(pltpu.VMEM(piece.shape, bf16),) * 2,
        in_specs=[SMEM] + [HBM] * 6,
        out_specs=(VMEM, VMEM),
        scratch_shapes=[pltpu.VMEM((TOK, TOK), bf16)] * 2
        + [pltpu.VMEM((1, TOK), f32)]
        + [pltpu.VMEM((TOK, TOK), bf16)] * 3
        + [pltpu.SemaphoreType.DMA((6,))],
        compiler_params=PARAMS,
    )(
        cores,
        far(keys),
        far(values),
        far(rates.reshape(1, TOK)),
        far(w_gate),
        far(w_up),
        far(w_down),
    )
    got = lax.ppermute(other, "seq", PARTNER)
    both = pl.pallas_call(
        pair_kernel,
        out_shape=pltpu.VMEM(piece.shape, bf16),
        in_specs=[VMEM] * 2,
        out_specs=VMEM,
        compiler_params=PARAMS,
    )(near_core(mine), near_core(got))
    came = lax.all_to_all(both, "seq", 0, 0, axis_index_groups=SAME_CORE)
    weights = [lax.dynamic_slice_in_dim(w, index * COLS, COLS, 1) for w in (w_gate, w_up, w_down)]
    weights = jnp.concatenate(weights, axis=1).T
    near_k = lax.ppermute(jnp.where(core == 0, keys, k2), "seq", PARTNER)
    near_v = lax.ppermute(jnp.where(core == 0, values, v2), "seq", PARTNER)
    attn = pl.pallas_call(
        attention_kernel,
        out_shape=jax.ShapeDtypeStruct((TOK, TOK), f32),
        in_specs=[SMEM, SMEM] + [HBM] * 7,
        out_specs=VMEM,
        scratch_shapes=[pltpu.VMEM((TOK, TOK), bf16)] * 7 + [pltpu.SemaphoreType.DMA((7,))],
        compiler_params=PARAMS,
    )(
        jnp.reshape(index * TOK, (1,)),
        lengths,
        far(queries),
        far(k2),
        far(v2),
        far(near_k),
        far(near_v),
        far(keys),
        far(values),
    )
    *news, spread = pl.pallas_call(
        update_kernel,
        out_shape=(jax.ShapeDtypeStruct((COLS, TOK), f32),) * 3
        + (pltpu.VMEM((CHIPS // 2, PART, TOK), bf16),),
        in_specs=[VMEM] * 2 + [HBM] * 3,
        out_specs=(VMEM,) * 4,
        scratch_shapes=[pltpu.VMEM((COLS, TOK), f32)] * 3 + [pltpu.SemaphoreType.DMA((3,))],
        compiler_params=PARAMS,
    )(near_core(came), near_core(weights), far(mom_gate.T), far(mom_up.T), far(mom_down.T))
    same = lax.all_to_all(spread, "seq", 0, 0, axis_index_groups=SAME_PARITY)
    to_right, to_left = pl.pallas_call(
        pick_kernel,
        out_shape=(pltpu.VMEM((2, PART, TOK), bf16),) * 2,
        in_specs=[SMEM, VMEM],
        out_specs=(VMEM,) * 2,
        compiler_params=PARAMS,
    )(chips, near_core(same))
    from_left = lax.ppermute(to_right, "seq", RIGHT)
    from_right = lax.ppermute(to_left, "seq", LEFT)
    same_swap = lax.ppermute(same, "seq", PARTNER)
    sides = jnp.concatenate((from_left, from_right), axis=0)
    sides_swap = lax.ppermute(sides, "seq", PARTNER)
    mixed = pl.pallas_call(
        fast_kernel,
        out_shape=jax.ShapeDtypeStruct((TOK, TOK), bf16),
        in_specs=[SMEM, SMEM] + [VMEM] * 7,
        out_specs=VMEM,
        compiler_params=PARAMS,
        scratch_shapes=[pltpu.VMEM((TOK, TOK), bf16)] * 3,
    )(
        cores,
        chips,
        *[near_core(x) for x in (queries, same, sides, same_swap, sides_swap, attn)],
        norm_gain.reshape(1, TOK),
    )
    return (mixed, *[new.T for new in news])


def solution(mesh):
    in_specs = (
        P(("doc", "seq"), None),
        P(("doc", "seq"), None),
        P(("doc", "seq"), None),
        P(("doc", "seq")),
        P("doc"),
        P("doc"),
        P("doc", None),
        P("doc", None),
        P("doc", None),
        P("doc", "seq"),
        P("doc", "seq"),
        P("doc", "seq"),
    )
    out_specs = (P(("doc", "seq"), None), P("doc", "seq"), P("doc", "seq"), P("doc", "seq"))
    return jax.shard_map(local, mesh=mesh, in_specs=in_specs, out_specs=out_specs, check_vma=False)
```

```python
import jax
import jax.numpy as jnp
from jax import lax
from jax.experimental import pallas as pl
from jax.experimental.pallas import tpu as pltpu
from jax.sharding import PartitionSpec as P

WIN = 1024
TOK = 512
CHIPS = 8
COLS = 32
PART = 3 * COLS
GRAD_SCALE = float(2 * CHIPS * TOK) ** (-0.5)

momentum_decay = 0.9
step_size = 0.5

PARTNER = [(i, i ^ 1) for i in range(2 * CHIPS)]
NEXT_CHIP = [(i, i + 2) for i in range(2 * CHIPS - 2)]
SAME_CORE = [[c + 2 * k for k in range(CHIPS)] for c in range(2)]

f32 = jnp.float32
bf16 = jnp.bfloat16


def contract(x, y, dims):
    return lax.dot_general(x, y, ((dims[:1], dims[1:]), ((), ())), preferred_element_type=f32)


def grads_kernel(core, keys, values, rates, w_gate, w_up, w_down, mine, other, *refs):
    bufs, sems = refs[:6], refs[6]
    copies = [
        pltpu.make_async_copy(src, dst, sems.at[n])
        for n, (src, dst) in enumerate(zip((keys, w_gate, rates, values, w_up, w_down), bufs))
    ]
    for copy in copies:
        copy.start()
    k_buf, gate_buf, rate_buf, v_buf, up_buf, down_buf = bufs
    copies[0].wait()
    copies[1].wait()
    k = k_buf[...]
    gate = contract(k, gate_buf[...], (1, 0))
    copies[2].wait()
    per_token = jnp.broadcast_to(rate_buf[...], (128, TOK)).T
    copies[3].wait()
    err = jnp.concatenate(
        [-(per_token * v_buf[:, i : i + 128].astype(f32)) for i in range(0, TOK, 128)], axis=1
    ).astype(bf16)
    copies[4].wait()
    upper = contract(k, up_buf[...], (1, 0))
    copies[5].wait()
    back = contract(err, down_buf[...], (1, 1))
    sig = jax.nn.sigmoid(gate)
    act = gate * sig
    slope = sig * (1.0 + gate * (1.0 - sig))
    hidden = (act * upper).astype(bf16)
    d_up = (back * act).astype(bf16)
    d_gate = (back * upper * slope).astype(bf16)
    for n, (x, y) in enumerate(((d_gate, k), (d_up, k), (err, hidden))):
        part = contract(x, y, (0, 0)).astype(bf16)
        rows = slice(n * COLS, (n + 1) * COLS)
        halves = [
            [part[(2 * d + c) * COLS : (2 * d + c + 1) * COLS] for d in range(CHIPS)] for c in range(2)
        ]
        for c in range(2):

            @pl.when(core[0] == c)
            def _():
                for d in range(CHIPS):
                    mine[d, rows] = halves[c][d]
                    other[d, rows] = halves[1 - c][d]


def pair_kernel(mine, got, out):
    for d in range(CHIPS):
        out[d] = (mine[d].astype(f32) + got[d].astype(f32)).astype(bf16)


def update_kernel(came, *refs):
    weights, moms, news, spread = refs[0], refs[1:4], refs[4:7], refs[7]
    bufs, sems = refs[8:11], refs[11]
    copies = [pltpu.make_async_copy(moms[n], bufs[n], sems.at[n]) for n in range(3)]
    for copy in copies:
        copy.start()
    for n in range(3):
        rows = slice(n * COLS, (n + 1) * COLS)
        total = came[0, rows].astype(f32)
        for d in range(1, CHIPS):
            total = total + came[d, rows].astype(f32)
        copies[n].wait()
        new = momentum_decay * bufs[n][...] + total * GRAD_SCALE
        news[n][...] = new
        normed = new * lax.rsqrt(jnp.sum(new * new, axis=1, keepdims=True) + 1e-06)
        shard = (weights[rows].astype(f32) - step_size * normed).astype(bf16)
        for d in range(CHIPS):
            spread[d, rows] = shard


BLOCK = 256


def attention_kernel(first, lengths, *refs):
    out, bufs, sems = refs[7], refs[8:15], refs[15]
    copies = [pltpu.make_async_copy(refs[n], bufs[n], sems.at[n]) for n in range(7)]
    for copy in copies:
        copy.start()
    for copy in copies:
        copy.wait()
    q, k2, v2, k1, v1, k0, v0 = bufs
    for b in range(TOK // BLOCK):
        qb = q[b * BLOCK : (b + 1) * BLOCK]
        qpos = first[0] + b * BLOCK + lax.broadcasted_iota(jnp.int32, (BLOCK, 1), 0)
        low = jnp.maximum(qpos - (WIN - 1), 0)
        end = 0
        for n in range(4):
            end = end + lengths[n]
            low = jnp.where(qpos >= end, jnp.maximum(low, end), low)
        pieces = []
        for hop, kref, vref in ((2, k2, v2), (1, k1, v1), (0, k0, v0)):
            lo = max(0, b * BLOCK - WIN + hop * TOK)
            hi = min(TOK, (b + 1) * BLOCK + hop * TOK)
            s = contract(qb, kref[lo:hi], (1, 1)) * (TOK ** (-0.5))
            kpos = first[0] - hop * TOK + lo + lax.broadcasted_iota(jnp.int32, (1, hi - lo), 1)
            s = jnp.where((kpos >= low) & (kpos <= qpos), s, -1e30)
            pieces.append((s, vref[lo:hi]))
        top = pieces[0][0].max(axis=1, keepdims=True)
        for s, _ in pieces[1:]:
            top = jnp.maximum(top, s.max(axis=1, keepdims=True))
        total = 0.0
        acc = 0.0
        for s, v in pieces:
            w = jnp.exp(s - top)
            total = total + w.sum(axis=1, keepdims=True)
            acc = acc + contract(w.astype(bf16), v, (1, 0))
        out[b * BLOCK : (b + 1) * BLOCK] = acc / total


def fast_kernel(core, q, same, swap, attn, gain, out, gate_t, up_t, down_t):
    for side, src in ((core[0], same), (1 - core[0], swap)):
        for d in range(CHIPS):
            at = pl.ds(pl.multiple_of((2 * d + side) * COLS, COLS), COLS)
            for n, dst in enumerate((gate_t, up_t, down_t)):
                dst[at, :] = src[d, n * COLS : (n + 1) * COLS]
    x = q[...]
    qa = contract(x, gate_t[...], (1, 1))
    qb = contract(x, up_t[...], (1, 1))
    qh = (qa * jax.nn.sigmoid(qa) * qb).astype(bf16)
    fast = contract(qh, down_t[...], (1, 1))
    scale = lax.rsqrt(jnp.mean(fast * fast, axis=1, keepdims=True) + 1e-06)
    out[...] = (attn[...] + fast * scale * gain[...]).astype(bf16)


def near_core(x):
    return pltpu.with_memory_space_constraint(x, pltpu.VMEM)


def far(x):
    return pltpu.with_memory_space_constraint(x, pltpu.HBM)


PARAMS = pltpu.CompilerParams(vmem_limit_bytes=24 * 2**20)
SMEM = pl.BlockSpec(memory_space=pltpu.SMEM)
VMEM = pl.BlockSpec(memory_space=pltpu.VMEM)
HBM = pl.BlockSpec(memory_space=pltpu.HBM)


def local(
    queries,
    keys,
    values,
    rates,
    lengths,
    norm_gain,
    w_gate,
    w_up,
    w_down,
    mom_gate,
    mom_up,
    mom_down,
):
    index = lax.axis_index("seq")
    core = index % 2
    cores = jnp.reshape(core, (1,))
    k2 = lax.ppermute(keys, "seq", NEXT_CHIP)
    v2 = lax.ppermute(values, "seq", NEXT_CHIP)
    piece = jax.ShapeDtypeStruct((CHIPS, PART, TOK), bf16)
    mine, other = pl.pallas_call(
        grads_kernel,
        out_shape=(pltpu.VMEM(piece.shape, bf16),) * 2,
        in_specs=[SMEM] + [HBM] * 6,
        out_specs=(VMEM, VMEM),
        scratch_shapes=[pltpu.VMEM((TOK, TOK), bf16)] * 2
        + [pltpu.VMEM((1, TOK), f32)]
        + [pltpu.VMEM((TOK, TOK), bf16)] * 3
        + [pltpu.SemaphoreType.DMA((6,))],
        compiler_params=PARAMS,
    )(
        cores,
        far(keys),
        far(values),
        far(rates.reshape(1, TOK)),
        far(w_gate),
        far(w_up),
        far(w_down),
    )
    got = lax.ppermute(other, "seq", PARTNER)
    both = pl.pallas_call(
        pair_kernel,
        out_shape=pltpu.VMEM(piece.shape, bf16),
        in_specs=[VMEM] * 2,
        out_specs=VMEM,
        compiler_params=PARAMS,
    )(near_core(mine), near_core(got))
    came = lax.all_to_all(both, "seq", 0, 0, axis_index_groups=SAME_CORE)
    weights = [lax.dynamic_slice_in_dim(w, index * COLS, COLS, 1) for w in (w_gate, w_up, w_down)]
    weights = jnp.concatenate(weights, axis=1).T
    near_k = lax.ppermute(jnp.where(core == 0, keys, k2), "seq", PARTNER)
    near_v = lax.ppermute(jnp.where(core == 0, values, v2), "seq", PARTNER)
    attn = pl.pallas_call(
        attention_kernel,
        out_shape=jax.ShapeDtypeStruct((TOK, TOK), f32),
        in_specs=[SMEM, SMEM] + [HBM] * 7,
        out_specs=VMEM,
        scratch_shapes=[pltpu.VMEM((TOK, TOK), bf16)] * 7 + [pltpu.SemaphoreType.DMA((7,))],
        compiler_params=PARAMS,
    )(
        jnp.reshape(index * TOK, (1,)),
        lengths,
        far(queries),
        far(k2),
        far(v2),
        far(near_k),
        far(near_v),
        far(keys),
        far(values),
    )
    *news, spread = pl.pallas_call(
        update_kernel,
        out_shape=(pltpu.VMEM((COLS, TOK), f32),) * 3 + (pltpu.VMEM(piece.shape, bf16),),
        in_specs=[VMEM] * 2 + [HBM] * 3,
        out_specs=(VMEM,) * 4,
        scratch_shapes=[pltpu.VMEM((COLS, TOK), f32)] * 3 + [pltpu.SemaphoreType.DMA((3,))],
        compiler_params=PARAMS,
    )(near_core(came), near_core(weights), far(mom_gate.T), far(mom_up.T), far(mom_down.T))
    same = lax.all_to_all(spread, "seq", 0, 0, axis_index_groups=SAME_CORE)
    swap = lax.ppermute(same, "seq", PARTNER)
    mixed = pl.pallas_call(
        fast_kernel,
        out_shape=jax.ShapeDtypeStruct((TOK, TOK), bf16),
        in_specs=[SMEM] + [VMEM] * 5,
        out_specs=VMEM,
        compiler_params=PARAMS,
        scratch_shapes=[pltpu.VMEM((TOK, TOK), bf16)] * 3,
    )(
        cores,
        near_core(queries),
        near_core(same),
        near_core(swap),
        near_core(attn),
        norm_gain.reshape(1, TOK),
    )
    return (mixed, *[new.T for new in news])


def solution(mesh):
    in_specs = (
        P(("doc", "seq"), None),
        P(("doc", "seq"), None),
        P(("doc", "seq"), None),
        P(("doc", "seq")),
        P("doc"),
        P("doc"),
        P("doc", None),
        P("doc", None),
        P("doc", None),
        P("doc", "seq"),
        P("doc", "seq"),
        P("doc", "seq"),
    )
    out_specs = (P(("doc", "seq"), None), P("doc", "seq"), P("doc", "seq"), P("doc", "seq"))
    return jax.shard_map(local, mesh=mesh, in_specs=in_specs, out_specs=out_specs, check_vma=False)
```
